32 devices in a mesh: gx: 4 (over z), gy: 2 (over y), gz: 4 (over x, core).
Axes of the slice: x: 2, y: 2, z: 4, core: 2. Of those that a mesh axis runs over, the one named last changes fastest.
Arguments:
- density: float32 [32, 16, 512], P('gx', 'gy', 'gz'), may hold values from 0.5 to 2
- base_velocity: float32 [3, 32, 16, 512], P(None, 'gx', 'gy', 'gz'), may hold values from -0.4 to 0.4
- cells: int32 [3, 8192], P(None, ('gx', 'gy', 'gz')), may hold values from 0 to 511, as said below
- offsets: float32 [3, 8192], P(None, ('gx', 'gy', 'gz')), may hold values from 0 to 1
- target: float32 [3, 8192], P(None, ('gx', 'gy', 'gz')), may hold values from -0.4 to 0.4
- stiffness: float32 [8192], P(('gx', 'gy', 'gz')), may hold values from 0.01 to 0.1
- counts: int32 [32], P(('gx', 'gy', 'gz')), may hold values from 1 to 256, as said below
Outputs:
- forces: float32 [3, 8192], P(None, ('gx', 'gy', 'gz'))
The draws below stay inside these ranges and needn't reach their ends.
Inputs may be any that keep to these rules, and one draw needn't show every extreme that they name: `cells`: each marker's cell lies inside the lattice block of the device that holds its slot. `counts`: some device holds exactly 256 live markers in every draw.
All inputs are finite; a program needn't handle non-finite values.
Results may differ from the reference program's by a relative error of at most 0.0001.
Values sent between devices are 32-bit elements; how exact they have to be, the bound alone decides.
A program may use at most 64 MiB of HBM per device.

```python
import math
import jax
import jax.numpy as jnp
from jax import lax

CX = 8
CY = 8
CZ = 128
CAP = 256
ITERS = 3
NX = 32
NY = 16
NZ = 512
SLOTS = 8192
DEVICES = 32


def draw_cells(key, part):
    blocks_y = NY // CY
    blocks_z = NZ // CZ
    device = jnp.arange(SLOTS, dtype=jnp.int32) // CAP
    block_x = device // (blocks_y * blocks_z)
    block_y = device // blocks_z % blocks_y
    block_z = device % blocks_z
    keys = jax.random.split(key, 3)
    inside_x = jax.random.randint(keys[0], (SLOTS,), 0, CX, dtype=jnp.int32)
    inside_y = jax.random.randint(keys[1], (SLOTS,), 0, CY, dtype=jnp.int32)
    inside_z = jax.random.randint(keys[2], (SLOTS,), 0, CZ, dtype=jnp.int32)
    return jnp.stack([block_x * CX + inside_x, block_y * CY + inside_y, block_z * CZ + inside_z]).astype(jnp.int32)


def draw_counts(key, part):
    keys = jax.random.split(key, 3)
    divisor = 1 + jax.random.randint(keys[0], (DEVICES,), 0, 6, dtype=jnp.int32)
    jitter = jax.random.randint(keys[1], (DEVICES,), 0, CAP // 8 + 1, dtype=jnp.int32)
    loads = jnp.maximum(CAP // divisor - jitter, 1)
    fullest = jax.random.randint(keys[2], (), 0, DEVICES, dtype=jnp.int32)
    loads = jnp.where(jnp.arange(DEVICES, dtype=jnp.int32) == fullest, CAP, loads)
    return loads.astype(jnp.int32)


def levels(stream_key, extent, shards, low, largest):
    level, own = 1.0, jax.random.fold_in(stream_key, 6)
    for axis_at, blocks in shards:
        steps = jnp.exp(jax.random.uniform(jax.random.fold_in(own, axis_at), (blocks,), jnp.float32, low / len(shards), largest / len(shards)))
        level = level * jnp.repeat(steps, extent[axis_at] // blocks).reshape([-1 if axis == axis_at else 1 for axis in range(len(extent))])
    return level


def normal_values(stream_key, dims, scale, limit, shards=(), kind=jnp.bfloat16):
    values = scale * jax.random.normal(stream_key, dims, jnp.float32)
    if shards:
        values = values * levels(stream_key, dims, shards, -0.22, 0.18)
    return jnp.clip(values, -limit, limit).astype(kind)


def setup_inputs(seed: int = 0) -> dict:
    seeds = jax.random.split(jax.random.key(seed), 8)
    return {
        "density": jnp.clip(jnp.exp(math.log(2.0) - 1.3862944 * jax.random.uniform(seeds[0], (NX, NY, NZ), jnp.float32) ** levels(seeds[0], (NX, NY, NZ), ((0, 4), (1, 2), (2, 4)), -0.2, 0.2)), 0.5, 2.0),
        "base_velocity": normal_values(seeds[1], (3, NX, NY, NZ), 0.05, 0.4, ((1, 4), (2, 2), (3, 4)), jnp.float32),
        "cells": draw_cells(jax.random.fold_in(seeds[7], 71), 0),
        "offsets": jnp.clip(1.0 * jax.random.uniform(seeds[3], (3, SLOTS), jnp.float32) ** levels(seeds[3], (3, SLOTS), ((1, 32),), -0.2, 0.2), 0.0, 1.0),
        "target": normal_values(seeds[4], (3, SLOTS), 0.05, 0.4, ((1, 32),), jnp.float32),
        "stiffness": jnp.clip(jnp.exp(math.log(0.1) - 2.3025851 * jax.random.uniform(seeds[5], (SLOTS,), jnp.float32) ** levels(seeds[5], (SLOTS,), ((0, 32),), -0.2, 0.2)), 0.01, 0.1),
        "counts": draw_counts(jax.random.fold_in(seeds[7], 71), 0),
    }


def moving_directions():
    listing = []
    for along_x in (-1, 0, 1):
        for along_y in (-1, 0, 1):
            for along_z in (-1, 0, 1):
                order = abs(along_x) + abs(along_y) + abs(along_z)
                if order == 1:
                    listing.append((along_x, along_y, along_z, 1.0 / 18.0))
                elif order == 2:
                    listing.append((along_x, along_y, along_z, 1.0 / 36.0))
    return listing

def delta_weights(fraction):

    def inner(radius):
        return (3.0 - 2.0 * radius + jnp.sqrt(1.0 + 4.0 * radius - 4.0 * radius * radius)) / 8.0

    def outer(radius):
        return (5.0 - 2.0 * radius - jnp.sqrt(-7.0 + 12.0 * radius - 4.0 * radius * radius)) / 8.0
    return jnp.stack([outer(1.0 + fraction), inner(fraction), inner(1.0 - fraction), outer(2.0 - fraction)])

def reference(density, base_velocity, cells, offsets, target, stiffness, counts):
    live = (jnp.arange(CAP, dtype=jnp.int32)[None, :] < counts[:, None]).reshape(-1).astype(jnp.float32)
    scale = lax.rsqrt(density)
    weight_x = delta_weights(offsets[0])
    weight_y = delta_weights(offsets[1])
    weight_z = delta_weights(offsets[2])
    index_x = [((cells[0] + shift - 1) % NX).astype(jnp.int32) for shift in range(4)]
    index_y = [((cells[1] + shift - 1) % NY).astype(jnp.int32) for shift in range(4)]
    index_z = [((cells[2] + shift - 1) % NZ).astype(jnp.int32) for shift in range(4)]
    directions = moving_directions()

    def interpolate(field):
        total = jnp.zeros((3, SLOTS), jnp.float32)
        for first in range(4):
            for second in range(4):
                for third in range(4):
                    weight = weight_x[first] * weight_y[second] * weight_z[third]
                    total = total + field[:, index_x[first], index_y[second], index_z[third]] * weight
        return total

    def spread(vector):
        grid = jnp.zeros((3, NX, NY, NZ), jnp.float32)
        for first in range(4):
            for second in range(4):
                for third in range(4):
                    weight = weight_x[first] * weight_y[second] * weight_z[third]
                    grid = grid.at[:, index_x[first], index_y[second], index_z[third]].add(vector * weight)
        return grid

    def apply(vector):
        moved = scale * spread(vector)
        post = [jnp.zeros((NX, NY, NZ), jnp.float32) for component in range(3)]
        for along_x, along_y, along_z, share in directions:
            population = 3.0 * share * (along_x * moved[0] + along_y * moved[1] + along_z * moved[2])
            shifted = jnp.roll(population, (along_x, along_y, along_z), axis=(0, 1, 2))
            for component, along in enumerate((along_x, along_y, along_z)):
                if along != 0:
                    post[component] = post[component] + along * shifted
        velocity = scale * (moved + jnp.stack(post)) * 0.5
        return live * (interpolate(velocity) + stiffness * vector)
    right = live * (target - interpolate(base_velocity))
    solution = jnp.zeros_like(right)
    residual = right
    direction = right
    norm_now = jnp.sum(residual * residual)
    for step in range(ITERS):
        image = apply(direction)
        alpha = norm_now / jnp.sum(direction * image)
        solution = solution + alpha * direction
        residual = residual - alpha * image
        norm_next = jnp.sum(residual * residual)
        direction = residual + norm_next / norm_now * direction
        norm_now = norm_next
    return solution
```

```python
import functools
import itertools

import jax
import jax.numpy as jnp
from jax import lax
from jax.experimental import pallas as pl
from jax.experimental.pallas import tpu as pltpu
from jax.sharding import PartitionSpec as P

ITERS = 3
LOW, HIGH = 2, 3
MESH_ID = pl.DeviceIdType.MESH
AXES = ("gx", "gy", "gz")


def round_up(value, multiple):
    return -(-value // multiple) * multiple


def extended(cells, sides):
    for axis, dim in sides:
        count = lax.axis_size(axis)
        head = lax.slice_in_dim(cells, 0, HIGH, axis=dim)
        tail = lax.slice_in_dim(cells, cells.shape[dim] - LOW, cells.shape[dim], axis=dim)
        cells = jnp.concatenate(
            [
                lax.ppermute(tail, axis, [(i, (i + 1) % count) for i in range(count)]),
                cells,
                lax.ppermute(head, axis, [((i + 1) % count, i) for i in range(count)]),
            ],
            axis=dim,
        )
    return cells


def axis_groups(count):
    groups = {}
    for shift in (0, -1, 1):
        groups.setdefault(shift % count, []).append(shift)
    return list(groups.items())


def span(shifts, size):
    if shifts == [0]:
        return 1, size + 3
    if shifts == [-1]:
        return 0, 4
    if shifts == [1]:
        return size + 1, 4
    return 0, size + 5


def weights(fraction):
    root = jnp.sqrt(1.0 + 4.0 * fraction - 4.0 * fraction * fraction)
    near, far = 3.0 - 2.0 * fraction, 1.0 + 2.0 * fraction
    return ((near - root) / 8.0, (near + root) / 8.0, (far + root) / 8.0, (far - root) / 8.0)


def table(cell, four, shifts, size, first, rows):
    place = lax.broadcasted_iota(jnp.int32, (rows, cell.shape[1]), 0).astype(jnp.float32) + first
    total = None
    for shift in shifts:
        apart = place - (cell + (1.0 + shift * size))
        part = jnp.where(apart == 3.0, four[3], 0.0)
        for number in (2, 1, 0):
            part = jnp.where(apart == float(number), four[number], part)
        total = part if total is None else total + part
    return total


def split(value):
    high = value.astype(jnp.bfloat16)
    return high, (value - high.astype(jnp.float32)).astype(jnp.bfloat16)


def dot_nt(a, b):
    return lax.dot_general(a, b, (((1,), (1,)), ((), ())), preferred_element_type=jnp.float32)


def dot_nn(a, b):
    return lax.dot_general(a, b, (((1,), (0,)), ((), ())), preferred_element_type=jnp.float32)


def kernel(
    counts, sizes, fields, marks, aux, out, nbuf, rbuf, txy, thi, tlo, whi, wlo, grid,
    nsend, nrecv, rsend, rrecv,
):
    size_x, size_y, size_z = sizes
    cap = marks.shape[1]
    rows_y, lanes = fields.shape[2], fields.shape[3]
    wide_x = size_x + 5
    groups = [axis_groups(count) for count in counts]
    slots = list(itertools.product(*[[offset for offset, _ in group] for group in groups]))
    me = [lax.axis_index(name) for name in AXES]
    sent = []

    def device(offset):
        return tuple(lax.rem(m + o, n) for m, o, n in zip(me, offset, counts))

    def negated(offset):
        return tuple((-o) % n for o, n in zip(offset, counts))

    peers = {slot for slot in slots if any(slot)}
    for axis, count in enumerate(counts):
        for step in range(1, count):
            peers.add(tuple(step if a == axis else 0 for a in range(3)))
    peers = sorted(peers)
    barrier = pltpu.get_barrier_semaphore()
    for peer in peers:
        pl.semaphore_signal(barrier, inc=1, device_id=device(peer), device_id_type=MESH_ID)
    pl.semaphore_wait(barrier, len(peers))

    def neighbour_copy(turn, number):
        return pltpu.make_async_remote_copy(
            src_ref=nbuf.at[turn, 0],
            dst_ref=nbuf.at[turn, number],
            send_sem=nsend.at[turn, number - 1],
            recv_sem=nrecv.at[turn, number - 1],
            device_id=device(negated(slots[number])),
            device_id_type=MESH_ID,
        )

    def send_round(turn):
        for number in range(1, len(slots)):
            copy = neighbour_copy(turn, number)
            copy.start()
            sent.append(copy)

    def wait_round(turn):
        for number in range(1, len(slots)):
            neighbour_copy(turn, number).wait_recv()

    def sum_copy(turn, stage, step):
        axis = 2 - stage
        offset = tuple((-step) % counts[axis] if a == axis else 0 for a in range(3))
        return pltpu.make_async_remote_copy(
            src_ref=rbuf.at[turn, stage, 0],
            dst_ref=rbuf.at[turn, stage, step],
            send_sem=rsend.at[turn, stage, step - 1],
            recv_sem=rrecv.at[turn, stage, step - 1],
            device_id=device(offset),
            device_id_type=MESH_ID,
        )

    def send_sum(turn, stage, value):
        rbuf[turn, stage, 0] = value
        for step in range(1, counts[2 - stage]):
            copy = sum_copy(turn, stage, step)
            copy.start()
            sent.append(copy)

    def wait_sum(turn, stage):
        for step in range(1, counts[2 - stage]):
            sum_copy(turn, stage, step).wait_recv()
        total = rbuf[turn, stage, 0]
        for step in range(1, counts[2 - stage]):
            total = total + rbuf[turn, stage, step]
        return total

    def put(turn, vector):
        for c in range(3):
            nbuf[turn, 0, pl.ds(c, 1), :] = vector[c : c + 1]

    nbuf[0, 0] = marks[...]
    send_round(0)

    def build(xi, yi, zi):
        number = slots.index((groups[0][xi][0], groups[1][yi][0], groups[2][zi][0]))
        info = nbuf[0, number]
        cells = [info[k : k + 1] for k in range(3)]
        fours = [weights(info[k + 3 : k + 4]) for k in range(3)]
        block = (yi * len(groups[2]) + zi) * cap
        start, planes = span(groups[0][xi][1], size_x)
        first = start // 8 * 8
        tall = round_up(start + planes - first, 8)
        tab_x = table(cells[0], fours[0], groups[0][xi][1], size_x, float(first), tall)
        tab_y = table(cells[1], fours[1], groups[1][yi][1], size_y, 0.0, rows_y)
        for plane in range(planes):
            at = start - first + plane
            txy[xi, pl.ds(plane * rows_y, rows_y), pl.ds(block, cap)] = tab_x[at : at + 1] * tab_y
        shifts = groups[2][zi][1]
        start, planes = span(shifts, size_z)
        first = start // 16 * 16
        tall = round_up(start + planes - first, 16)
        tab_z = table(cells[2], fours[2], shifts, size_z, float(first), tall)
        high, low = split(tab_z)
        for ref, part in ((thi, high), (tlo, low)):
            if first:
                ref[xi, pl.ds(0, first), pl.ds(block, cap)] = jnp.zeros((first, cap), jnp.bfloat16)
            ref[xi, pl.ds(first, tall), pl.ds(block, cap)] = part
            rest = lanes - first - tall
            if rest:
                ref[xi, pl.ds(first + tall, rest), pl.ds(block, cap)] = jnp.zeros(
                    (rest, cap), jnp.bfloat16
                )

    start_own, planes_own = span(groups[0][0][1], size_x)

    def interpolate(field):
        rows = planes_own * rows_y
        high, low = split(field.reshape(3 * rows, lanes))
        z_high, z_low = thi[0, :, pl.ds(0, cap)], tlo[0, :, pl.ds(0, cap)]
        part = dot_nn(high, z_high) + dot_nn(low, z_high) + dot_nn(high, z_low)
        plane = txy[0, pl.ds(0, rows), pl.ds(0, cap)]
        return jnp.concatenate(
            [
                jnp.sum(part[c * rows : (c + 1) * rows] * plane, axis=0, keepdims=True)
                for c in range(3)
            ],
            axis=0,
        )

    def spread(turn):
        for xi, (off_x, shifts) in enumerate(groups[0]):
            start, planes = span(shifts, size_x)
            rows = planes * rows_y
            for yi, (off_y, _) in enumerate(groups[1]):
                for zi, (off_z, _) in enumerate(groups[2]):
                    number = slots.index((off_x, off_y, off_z))
                    block = (yi * len(groups[2]) + zi) * cap
                    plane = txy[xi, pl.ds(0, rows), pl.ds(block, cap)]
                    for c in range(3):
                        high, low = split(plane * nbuf[turn, number, pl.ds(c, 1), :])
                        whi[pl.ds(c * rows, rows), pl.ds(block, cap)] = high
                        wlo[pl.ds(c * rows, rows), pl.ds(block, cap)] = low
            high, low = whi[pl.ds(0, 3 * rows), :], wlo[pl.ds(0, 3 * rows), :]
            part = dot_nt(high, thi[xi]) + dot_nt(low, thi[xi]) + dot_nt(high, tlo[xi])
            part = part.reshape(3, planes, rows_y, lanes)
            if xi == 0:
                if start > 0:
                    grid[:, pl.ds(0, start)] = jnp.zeros((3, start, rows_y, lanes), jnp.float32)
                rest = wide_x - start - planes
                if rest > 0:
                    grid[:, pl.ds(start + planes, rest)] = jnp.zeros(
                        (3, rest, rows_y, lanes), jnp.float32
                    )
                grid[:, pl.ds(start, planes)] = part
            else:
                grid[:, pl.ds(start, planes)] += part

    def shifted(value, by, axis):
        return pltpu.roll(value, by % value.shape[axis], axis)

    def both(value, axis):
        return shifted(value, -1, axis), shifted(value, 1, axis)

    def add(value, axis):
        up, down = both(value, axis)
        return up + down

    def sub(value, axis):
        up, down = both(value, axis)
        return up - down

    def respond():
        scale = fields[3]
        mx, my, mz = (scale * grid[c] for c in range(3))
        slope_y, slope_z = sub(my, 1), sub(mz, 2)
        sum_x = 2.0 * mx + add(mx, 1) + add(mx, 2)
        slope = slope_y + slope_z
        px = sum_x[2:] + sum_x[:-2] + slope[2:] - slope[:-2]
        slope_x = mx[2:] - mx[:-2]
        sum_y = (2.0 * my + add(my, 2))[1:-1] + my[2:] + my[:-2]
        py = add(sum_y, 1) + sub(slope_x + slope_z[1:-1], 1)
        sum_z = (2.0 * mz + add(mz, 1))[1:-1] + mz[2:] + mz[:-2]
        pz = add(sum_z, 2) + sub(slope_x + slope_y[1:-1], 2)
        half = scale[1:-1] * 0.5
        return jnp.stack(
            [half * (m[1:-1] + p * (1.0 / 12.0)) for m, p in ((mx, px), (my, py), (mz, pz))]
        )

    target, stiffness, live = aux[pl.ds(0, 3), :], aux[pl.ds(3, 1), :], aux[pl.ds(4, 1), :]

    def apply(turn, vector, summing=None):
        wait_round(turn)
        spread(turn)
        if summing is not None:
            send_sum(summing, 1, wait_sum(summing, 0))
        field = respond()
        if summing is not None:
            send_sum(summing, 2, wait_sum(summing, 1))
        return live * (interpolate(field) + stiffness * vector)

    def partial_sums(residual, image):
        folded = []
        for other in (residual, image):
            row = jnp.sum(residual * other, axis=0, keepdims=True)
            total = row[:, :128]
            for at in range(128, cap, 128):
                total = total + row[:, at : at + 128]
            folded.append(total)
        which = lax.broadcasted_iota(jnp.int32, (8, 128), 0)
        return jnp.where(which == 0, folded[0], jnp.where(which == 1, folded[1], 0.0))

    def totals(turn):
        tile = wait_sum(turn, 2)
        return (
            jnp.sum(tile[0:1], axis=1, keepdims=True),
            jnp.sum(tile[1:2], axis=1, keepdims=True),
        )

    build(0, 0, 0)
    residual = live * (target - interpolate(fields[pl.ds(0, 3), pl.ds(1, size_x + 3)]))
    put(1, residual)
    send_round(1)
    wait_round(0)
    for xi, yi, zi in itertools.product(*[range(len(group)) for group in groups]):
        if (xi, yi, zi) != (0, 0, 0):
            build(xi, yi, zi)

    image = apply(1, residual)
    direction, along, along_image = residual, image, None
    answer = None
    norm_before = alpha = None
    for step in range(ITERS):
        send_sum(step, 0, partial_sums(residual, image))
        if step + 1 < ITERS:
            put(step + 2, image)
            send_round(step + 2)
            ahead = apply(step + 2, image, step)
        else:
            send_sum(step, 1, wait_sum(step, 0))
            send_sum(step, 2, wait_sum(step, 1))
        norm, product = totals(step)
        if step == 0:
            alpha = norm / product
            along_image = ahead
        else:
            ratio = norm / norm_before
            alpha = norm / (product - ratio * norm / alpha)
            direction = residual + ratio * direction
            if step + 1 < ITERS:
                along = image + ratio * along
                along_image = ahead + ratio * along_image
        answer = alpha * direction if answer is None else answer + alpha * direction
        norm_before = norm
        if step + 1 < ITERS:
            residual = residual - alpha * along
            image = image - alpha * along_image
    out[...] = answer
    for copy in sent:
        copy.wait_send()


def body(mesh_counts, density, base_velocity, cells, offsets, target, stiffness, counts):
    sizes = density.shape
    size_x, size_y, size_z = sizes
    cap = cells.shape[1]
    rows_y, lanes = round_up(size_y + 5, 16), round_up(size_z + 5, 128)
    anchor = jnp.stack([lax.axis_index(name) * size for name, size in zip(AXES, sizes)])
    local = (cells - anchor[:, None]).astype(jnp.float32)
    marks = jnp.concatenate([local, offsets, jnp.zeros((2, cap), jnp.float32)], axis=0)
    live = (jnp.arange(cap, dtype=jnp.int32) < counts[0]).astype(jnp.float32)
    aux = jnp.concatenate(
        [target, stiffness[None], live[None], jnp.zeros((3, cap), jnp.float32)], axis=0
    )
    stacked = jnp.concatenate([base_velocity, lax.rsqrt(density)[None]], axis=0)
    fields = extended(stacked, (("gz", 3), ("gy", 2), ("gx", 1)))
    fields = jnp.pad(
        fields, ((0, 0), (0, 0), (0, rows_y - size_y - 5), (0, lanes - size_z - 5))
    )
    groups = [axis_groups(count) for count in mesh_counts]
    number = len(groups[0]) * len(groups[1]) * len(groups[2])
    width = len(groups[1]) * len(groups[2]) * cap
    tallest = max(span(shifts, size_x)[1] for _, shifts in groups[0])
    longest = max(mesh_counts)
    turns = ITERS + 1
    return pl.pallas_call(
        functools.partial(kernel, mesh_counts, sizes),
        out_shape=jax.ShapeDtypeStruct((3, cap), jnp.float32),
        in_specs=[pl.BlockSpec(memory_space=pltpu.VMEM)] * 3,
        out_specs=pl.BlockSpec(memory_space=pltpu.VMEM),
        scratch_shapes=[
            pltpu.VMEM((turns, number, 8, cap), jnp.float32),
            pltpu.VMEM((ITERS, 3, longest, 8, 128), jnp.float32),
            pltpu.VMEM((len(groups[0]), tallest * rows_y, width), jnp.float32),
            pltpu.VMEM((len(groups[0]), lanes, width), jnp.bfloat16),
            pltpu.VMEM((len(groups[0]), lanes, width), jnp.bfloat16),
            pltpu.VMEM((3 * tallest * rows_y, width), jnp.bfloat16),
            pltpu.VMEM((3 * tallest * rows_y, width), jnp.bfloat16),
            pltpu.VMEM((3, size_x + 5, rows_y, lanes), jnp.float32),
            pltpu.SemaphoreType.DMA((turns, number - 1)),
            pltpu.SemaphoreType.DMA((turns, number - 1)),
            pltpu.SemaphoreType.DMA((ITERS, 3, longest - 1)),
            pltpu.SemaphoreType.DMA((ITERS, 3, longest - 1)),
        ],
        compiler_params=pltpu.CompilerParams(
            collective_id=0, has_side_effects=True, vmem_limit_bytes=60 * 1024 * 1024
        ),
    )(fields, marks, aux)


def solution(mesh):
    return jax.shard_map(
        functools.partial(body, tuple(mesh.shape[name] for name in AXES)),
        mesh=mesh,
        in_specs=(
            P("gx", "gy", "gz"),
            P(None, "gx", "gy", "gz"),
            P(None, ("gx", "gy", "gz")),
            P(None, ("gx", "gy", "gz")),
            P(None, ("gx", "gy", "gz")),
            P(("gx", "gy", "gz")),
            P(("gx", "gy", "gz")),
        ),
        out_specs=P(None, ("gx", "gy", "gz")),
        check_vma=False,
    )
```

```python
import functools
import itertools

import jax
import jax.numpy as jnp
from jax import lax
from jax.experimental import pallas as pl
from jax.experimental.pallas import tpu as pltpu
from jax.sharding import PartitionSpec as P

ITERS = 3
MOST_DIRECT = 64
LOW, HIGH = 2, 3
MESH_ID = pl.DeviceIdType.MESH
AXES = ("gx", "gy", "gz")


def round_up(value, multiple):
    return -(-value // multiple) * multiple


def extended(cells, sides):
    for axis, dim in sides:
        count = lax.axis_size(axis)
        head = lax.slice_in_dim(cells, 0, HIGH, axis=dim)
        tail = lax.slice_in_dim(cells, cells.shape[dim] - LOW, cells.shape[dim], axis=dim)
        cells = jnp.concatenate(
            [
                lax.ppermute(tail, axis, [(i, (i + 1) % count) for i in range(count)]),
                cells,
                lax.ppermute(head, axis, [((i + 1) % count, i) for i in range(count)]),
            ],
            axis=dim,
        )
    return cells


def axis_groups(count):
    groups = {}
    for shift in (0, -1, 1):
        groups.setdefault(shift % count, []).append(shift)
    return list(groups.items())


def span(shifts, size):
    if shifts == [0]:
        return 1, size + 3
    if shifts == [-1]:
        return 0, 4
    if shifts == [1]:
        return size + 1, 4
    return 0, size + 5


def weights(fraction):
    root = jnp.sqrt(1.0 + 4.0 * fraction - 4.0 * fraction * fraction)
    near, far = 3.0 - 2.0 * fraction, 1.0 + 2.0 * fraction
    return ((near - root) / 8.0, (near + root) / 8.0, (far + root) / 8.0, (far - root) / 8.0)


def table(cell, four, shifts, size, first, rows):
    place = lax.broadcasted_iota(jnp.int32, (rows, cell.shape[1]), 0).astype(jnp.float32) + first
    total = None
    for shift in shifts:
        apart = place - (cell + (1.0 + shift * size))
        part = jnp.where(apart == 3.0, four[3], 0.0)
        for number in (2, 1, 0):
            part = jnp.where(apart == float(number), four[number], part)
        total = part if total is None else total + part
    return total


def split(value):
    high = value.astype(jnp.bfloat16)
    return high, (value - high.astype(jnp.float32)).astype(jnp.bfloat16)


def dot_nt(a, b):
    return lax.dot_general(a, b, (((1,), (1,)), ((), ())), preferred_element_type=jnp.float32)


def dot_nn(a, b):
    return lax.dot_general(a, b, (((1,), (0,)), ((), ())), preferred_element_type=jnp.float32)


def kernel(
    counts, sizes, fields, marks, aux, out, nbuf, fbuf, rbuf, dbuf, txy, thi, tlo, whi, wlo, grid,
    nsend, nrecv, rsend, rrecv, dsend, drecv,
):
    size_x, size_y, size_z = sizes
    cap = marks.shape[1]
    rows_y, lanes = fields.shape[2], fields.shape[3]
    wide_x = size_x + 5
    groups = [axis_groups(count) for count in counts]
    slots = list(itertools.product(*[[offset for offset, _ in group] for group in groups]))
    me = [lax.axis_index(name) for name in AXES]
    sent = []

    def device(offset):
        return tuple(lax.rem(m + o, n) for m, o, n in zip(me, offset, counts))

    def negated(offset):
        return tuple((-o) % n for o, n in zip(offset, counts))

    peers = {slot for slot in slots if any(slot)}
    for axis, count in enumerate(counts):
        for step in range(1, count):
            peers.add(tuple(step if a == axis else 0 for a in range(3)))
    everyone = [o for o in itertools.product(*[range(n) for n in counts]) if any(o)]
    direct = len(everyone) < MOST_DIRECT
    peers = everyone if direct else sorted(peers)
    barrier = pltpu.get_barrier_semaphore()
    for peer in peers:
        pl.semaphore_signal(barrier, inc=1, device_id=device(peer), device_id_type=MESH_ID)
    pl.semaphore_wait(barrier, len(peers))

    def neighbour_copy(turn, number):
        return pltpu.make_async_remote_copy(
            src_ref=fbuf.at[turn - 1, 0] if turn else nbuf.at[0],
            dst_ref=fbuf.at[turn - 1, number] if turn else nbuf.at[number],
            send_sem=nsend.at[turn, number - 1],
            recv_sem=nrecv.at[turn, number - 1],
            device_id=device(negated(slots[number])),
            device_id_type=MESH_ID,
        )

    def send_round(turn):
        for number in sorted(range(1, len(slots)), key=lambda k: (slots[k][0] == 0, k)):
            copy = neighbour_copy(turn, number)
            copy.start()
            sent.append(copy)

    def wait_round(turn, off_x):
        for number in range(1, len(slots)):
            if slots[number][0] == off_x:
                neighbour_copy(turn, number).wait_recv()

    def sum_copy(turn, stage, step):
        axis = 2 - stage
        offset = tuple((-step) % counts[axis] if a == axis else 0 for a in range(3))
        return pltpu.make_async_remote_copy(
            src_ref=rbuf.at[turn, stage, 0],
            dst_ref=rbuf.at[turn, stage, step],
            send_sem=rsend.at[turn, stage, step - 1],
            recv_sem=rrecv.at[turn, stage, step - 1],
            device_id=device(offset),
            device_id_type=MESH_ID,
        )

    def send_sum(turn, stage, value):
        rbuf[turn, stage, 0] = value
        for step in range(1, counts[2 - stage]):
            copy = sum_copy(turn, stage, step)
            copy.start()
            sent.append(copy)

    def wait_sum(turn, stage):
        for step in range(1, counts[2 - stage]):
            sum_copy(turn, stage, step).wait_recv()
        total = rbuf[turn, stage, 0]
        for step in range(1, counts[2 - stage]):
            total = total + rbuf[turn, stage, step]
        return total

    def put(turn, vector):
        for c in range(3):
            for part in range(cap // 128):
                fbuf[turn - 1, 0, pl.ds(c * (cap // 128) + part, 1), :] = vector[
                    c : c + 1, part * 128 : part * 128 + 128
                ]

    def taken(turn, number, c):
        each = cap // 128
        return jnp.concatenate(
            [fbuf[turn - 1, number, pl.ds(c * each + part, 1), :] for part in range(each)], axis=1
        )

    def direct_copy(number):
        return pltpu.make_async_remote_copy(
            src_ref=dbuf.at[0],
            dst_ref=dbuf.at[number + 1],
            send_sem=dsend.at[number],
            recv_sem=drecv.at[number],
            device_id=device(negated(everyone[number])),
            device_id_type=MESH_ID,
        )

    def sum_directly(value):
        dbuf[0] = value
        for number in range(len(everyone)):
            copy = direct_copy(number)
            copy.start()
            sent.append(copy)
        for number in range(len(everyone)):
            direct_copy(number).wait_recv()
        return jnp.sum(dbuf[...], axis=0)

    nbuf[0] = marks[...]
    send_round(0)

    def build(xi, yi, zi):
        number = slots.index((groups[0][xi][0], groups[1][yi][0], groups[2][zi][0]))
        info = nbuf[number]
        cells = [info[k : k + 1] for k in range(3)]
        fours = [weights(info[k + 3 : k + 4]) for k in range(3)]
        block = (yi * len(groups[2]) + zi) * cap
        start, planes = span(groups[0][xi][1], size_x)
        first = start // 8 * 8
        tall = round_up(start + planes - first, 8)
        tab_x = table(cells[0], fours[0], groups[0][xi][1], size_x, float(first), tall)
        tab_y = table(cells[1], fours[1], groups[1][yi][1], size_y, 0.0, rows_y)
        for plane in range(planes):
            at = start - first + plane
            txy[xi, pl.ds(plane * rows_y, rows_y), pl.ds(block, cap)] = tab_x[at : at + 1] * tab_y
        shifts = groups[2][zi][1]
        start, planes = span(shifts, size_z)
        first = start // 16 * 16
        tall = round_up(start + planes - first, 16)
        tab_z = table(cells[2], fours[2], shifts, size_z, float(first), tall)
        high, low = split(tab_z)
        for ref, part in ((thi, high), (tlo, low)):
            if first:
                ref[xi, pl.ds(0, first), pl.ds(block, cap)] = jnp.zeros((first, cap), jnp.bfloat16)
            ref[xi, pl.ds(first, tall), pl.ds(block, cap)] = part
            rest = lanes - first - tall
            if rest:
                ref[xi, pl.ds(first + tall, rest), pl.ds(block, cap)] = jnp.zeros(
                    (rest, cap), jnp.bfloat16
                )

    start_own, planes_own = span(groups[0][0][1], size_x)

    def interpolate(field):
        rows = planes_own * rows_y
        high, low = split(field.reshape(3 * rows, lanes))
        z_high, z_low = thi[0, :, pl.ds(0, cap)], tlo[0, :, pl.ds(0, cap)]
        part = dot_nn(high, z_high) + dot_nn(low, z_high) + dot_nn(high, z_low)
        plane = txy[0, pl.ds(0, rows), pl.ds(0, cap)]
        return jnp.concatenate(
            [
                jnp.sum(part[c * rows : (c + 1) * rows] * plane, axis=0, keepdims=True)
                for c in range(3)
            ],
            axis=0,
        )

    def spread(turn):
        for xi, (off_x, shifts) in enumerate(groups[0]):
            start, planes = span(shifts, size_x)
            rows = planes * rows_y
            wait_round(turn, off_x)
            for yi, (off_y, _) in enumerate(groups[1]):
                for zi, (off_z, _) in enumerate(groups[2]):
                    number = slots.index((off_x, off_y, off_z))
                    block = (yi * len(groups[2]) + zi) * cap
                    plane = txy[xi, pl.ds(0, rows), pl.ds(block, cap)]
                    for c in range(3):
                        high, low = split(plane * taken(turn, number, c))
                        whi[pl.ds(c * rows, rows), pl.ds(block, cap)] = high
                        wlo[pl.ds(c * rows, rows), pl.ds(block, cap)] = low
            high, low = whi[pl.ds(0, 3 * rows), :], wlo[pl.ds(0, 3 * rows), :]
            part = dot_nt(high, thi[xi]) + dot_nt(low, thi[xi]) + dot_nt(high, tlo[xi])
            part = part.reshape(3, planes, rows_y, lanes)
            if xi == 0:
                if start > 0:
                    grid[:, pl.ds(0, start)] = jnp.zeros((3, start, rows_y, lanes), jnp.float32)
                rest = wide_x - start - planes
                if rest > 0:
                    grid[:, pl.ds(start + planes, rest)] = jnp.zeros(
                        (3, rest, rows_y, lanes), jnp.float32
                    )
                grid[:, pl.ds(start, planes)] = part
            else:
                grid[:, pl.ds(start, planes)] += part

    def shifted(value, by, axis):
        return pltpu.roll(value, by % value.shape[axis], axis)

    def both(value, axis):
        return shifted(value, -1, axis), shifted(value, 1, axis)

    def add(value, axis):
        up, down = both(value, axis)
        return up + down

    def sub(value, axis):
        up, down = both(value, axis)
        return up - down

    def respond():
        scale = fields[3]
        mx, my, mz = (scale * grid[c] for c in range(3))
        slope_y, slope_z = sub(my, 1), sub(mz, 2)
        sum_x = 2.0 * mx + add(mx, 1) + add(mx, 2)
        slope = slope_y + slope_z
        px = sum_x[2:] + sum_x[:-2] + slope[2:] - slope[:-2]
        slope_x = mx[2:] - mx[:-2]
        sum_y = (2.0 * my + add(my, 2))[1:-1] + my[2:] + my[:-2]
        py = add(sum_y, 1) + sub(slope_x + slope_z[1:-1], 1)
        sum_z = (2.0 * mz + add(mz, 1))[1:-1] + mz[2:] + mz[:-2]
        pz = add(sum_z, 2) + sub(slope_x + slope_y[1:-1], 2)
        half = scale[1:-1] * 0.5
        return jnp.stack(
            [half * (m[1:-1] + p * (1.0 / 12.0)) for m, p in ((mx, px), (my, py), (mz, pz))]
        )

    target, stiffness, live = aux[pl.ds(0, 3), :], aux[pl.ds(3, 1), :], aux[pl.ds(4, 1), :]

    def apply(turn, vector, summing=None):
        spread(turn)
        if summing is not None:
            send_sum(summing, 1, wait_sum(summing, 0))
        field = respond()
        if summing is not None:
            send_sum(summing, 2, wait_sum(summing, 1))
        return live * (interpolate(field) + stiffness * vector)

    def partial_sums(residual, image):
        folded = []
        for other in (residual, image):
            row = jnp.sum(residual * other, axis=0, keepdims=True)
            total = row[:, :128]
            for at in range(128, cap, 128):
                total = total + row[:, at : at + 128]
            folded.append(total)
        return jnp.concatenate(folded, axis=0)

    def totals(tile):
        return (
            jnp.sum(tile[0:1], axis=1, keepdims=True),
            jnp.sum(tile[1:2], axis=1, keepdims=True),
        )

    build(0, 0, 0)
    residual = live * (target - interpolate(fields[pl.ds(0, 3), pl.ds(1, size_x + 3)]))
    put(1, residual)
    send_round(1)
    for off_x, _ in groups[0]:
        wait_round(0, off_x)
    for xi, yi, zi in itertools.product(*[range(len(group)) for group in groups]):
        if (xi, yi, zi) != (0, 0, 0):
            build(xi, yi, zi)

    image = apply(1, residual)
    direction, along, along_image = residual, image, None
    answer = None
    norm_before = alpha = None
    for step in range(ITERS):
        sums = partial_sums(residual, image)
        if step + 1 < ITERS or not direct:
            send_sum(step, 0, sums)
        if step + 1 < ITERS:
            put(step + 2, image)
            send_round(step + 2)
            ahead = apply(step + 2, image, step)
            norm, product = totals(wait_sum(step, 2))
        elif direct:
            norm, product = totals(sum_directly(sums))
        else:
            send_sum(step, 1, wait_sum(step, 0))
            send_sum(step, 2, wait_sum(step, 1))
            norm, product = totals(wait_sum(step, 2))
        if step == 0:
            alpha = norm / product
            along_image = ahead
        else:
            ratio = norm / norm_before
            alpha = norm / (product - ratio * norm / alpha)
            direction = residual + ratio * direction
            if step + 1 < ITERS:
                along = image + ratio * along
                along_image = ahead + ratio * along_image
        answer = alpha * direction if answer is None else answer + alpha * direction
        norm_before = norm
        if step + 1 < ITERS:
            residual = residual - alpha * along
            image = image - alpha * along_image
    out[...] = answer
    for copy in sent:
        copy.wait_send()


def body(mesh_counts, density, base_velocity, cells, offsets, target, stiffness, counts):
    sizes = density.shape
    size_x, size_y, size_z = sizes
    cap = cells.shape[1]
    rows_y, lanes = round_up(size_y + 5, 16), round_up(size_z + 5, 128)
    anchor = jnp.stack([lax.axis_index(name) * size for name, size in zip(AXES, sizes)])
    local = (cells - anchor[:, None]).astype(jnp.float32)
    marks = jnp.concatenate([local, offsets, jnp.zeros((2, cap), jnp.float32)], axis=0)
    live = (jnp.arange(cap, dtype=jnp.int32) < counts[0]).astype(jnp.float32)
    aux = jnp.concatenate(
        [target, stiffness[None], live[None], jnp.zeros((3, cap), jnp.float32)], axis=0
    )
    stacked = jnp.concatenate([base_velocity, lax.rsqrt(density)[None]], axis=0)
    fields = extended(stacked, (("gz", 3), ("gy", 2), ("gx", 1)))
    fields = jnp.pad(
        fields, ((0, 0), (0, 0), (0, rows_y - size_y - 5), (0, lanes - size_z - 5))
    )
    groups = [axis_groups(count) for count in mesh_counts]
    number = len(groups[0]) * len(groups[1]) * len(groups[2])
    width = len(groups[1]) * len(groups[2]) * cap
    tallest = max(span(shifts, size_x)[1] for _, shifts in groups[0])
    longest = max(mesh_counts)
    turns = ITERS + 1
    devices = mesh_counts[0] * mesh_counts[1] * mesh_counts[2]
    most = devices if devices <= MOST_DIRECT else 1
    return pl.pallas_call(
        functools.partial(kernel, mesh_counts, sizes),
        out_shape=jax.ShapeDtypeStruct((3, cap), jnp.float32),
        in_specs=[pl.BlockSpec(memory_space=pltpu.VMEM)] * 3,
        out_specs=pl.BlockSpec(memory_space=pltpu.VMEM),
        scratch_shapes=[
            pltpu.VMEM((number, 8, cap), jnp.float32),
            pltpu.VMEM((ITERS, number, 3 * (cap // 128), 128), jnp.float32),
            pltpu.VMEM((ITERS, 3, longest, 2, 128), jnp.float32),
            pltpu.VMEM((most, 2, 128), jnp.float32),
            pltpu.VMEM((len(groups[0]), tallest * rows_y, width), jnp.float32),
            pltpu.VMEM((len(groups[0]), lanes, width), jnp.bfloat16),
            pltpu.VMEM((len(groups[0]), lanes, width), jnp.bfloat16),
            pltpu.VMEM((3 * tallest * rows_y, width), jnp.bfloat16),
            pltpu.VMEM((3 * tallest * rows_y, width), jnp.bfloat16),
            pltpu.VMEM((3, size_x + 5, rows_y, lanes), jnp.float32),
            pltpu.SemaphoreType.DMA((turns, number - 1)),
            pltpu.SemaphoreType.DMA((turns, number - 1)),
            pltpu.SemaphoreType.DMA((ITERS, 3, longest - 1)),
            pltpu.SemaphoreType.DMA((ITERS, 3, longest - 1)),
            pltpu.SemaphoreType.DMA((most,)),
            pltpu.SemaphoreType.DMA((most,)),
        ],
        compiler_params=pltpu.CompilerParams(
            collective_id=0, has_side_effects=True, vmem_limit_bytes=60 * 1024 * 1024
        ),
    )(fields, marks, aux)


def solution(mesh):
    return jax.shard_map(
        functools.partial(body, tuple(mesh.shape[name] for name in AXES)),
        mesh=mesh,
        in_specs=(
            P("gx", "gy", "gz"),
            P(None, "gx", "gy", "gz"),
            P(None, ("gx", "gy", "gz")),
            P(None, ("gx", "gy", "gz")),
            P(None, ("gx", "gy", "gz")),
            P(("gx", "gy", "gz")),
            P(("gx", "gy", "gz")),
        ),
        out_specs=P(None, ("gx", "gy", "gz")),
        check_vma=False,
    )
```

```python
import functools
import itertools

import jax
import jax.numpy as jnp
from jax import lax
from jax.experimental import pallas as pl
from jax.experimental.pallas import tpu as pltpu
from jax.sharding import PartitionSpec as P

ITERS = 3
MOST_DIRECT = 64
LOW, HIGH = 2, 3
MESH_ID = pl.DeviceIdType.MESH
AXES = ("gx", "gy", "gz")


def round_up(value, multiple):
    return -(-value // multiple) * multiple


def axis_groups(count):
    groups = {}
    for shift in (0, -1, 1):
        groups.setdefault(shift % count, []).append(shift)
    return list(groups.items())


def span(shifts, size):
    if shifts == [0]:
        return 1, size + 3
    if shifts == [-1]:
        return 0, 4
    if shifts == [1]:
        return size + 1, 4
    return 0, size + 5


def weights(fraction):
    root = jnp.sqrt(1.0 + 4.0 * fraction - 4.0 * fraction * fraction)
    near, far = 3.0 - 2.0 * fraction, 1.0 + 2.0 * fraction
    return ((near - root) / 8.0, (near + root) / 8.0, (far + root) / 8.0, (far - root) / 8.0)


def table(cell, four, shifts, size, first, rows):
    place = lax.broadcasted_iota(jnp.int32, (rows, cell.shape[1]), 0).astype(jnp.float32) + first
    total = None
    for shift in shifts:
        apart = place - (cell + (1.0 + shift * size))
        part = jnp.where(apart == 3.0, four[3], 0.0)
        for number in (2, 1, 0):
            part = jnp.where(apart == float(number), four[number], part)
        total = part if total is None else total + part
    return total


def split(value):
    high = value.astype(jnp.bfloat16)
    return high, (value - high.astype(jnp.float32)).astype(jnp.bfloat16)


def dot_nt(a, b):
    return lax.dot_general(a, b, (((1,), (1,)), ((), ())), preferred_element_type=jnp.float32)


def dot_nn(a, b):
    return lax.dot_general(a, b, (((1,), (0,)), ((), ())), preferred_element_type=jnp.float32)


def kernel(
    counts, sizes, block, marks, aux, out, fields, xbuf, ybuf, zpack, zbuf, nbuf, fbuf, rbuf, dbuf, txy, thi, tlo, whi, wlo, grid,
    nsend, nrecv, rsend, rrecv, dsend, drecv, hsend, hrecv,
):
    size_x, size_y, size_z = sizes
    cap = marks.shape[1]
    rows_y, lanes = fields.shape[2], fields.shape[3]
    assert 8 * (size_x + 5) <= size_z == lanes - size_z
    wide_x = size_x + 5
    groups = [axis_groups(count) for count in counts]
    slots = list(itertools.product(*[[offset for offset, _ in group] for group in groups]))
    me = [lax.axis_index(name) for name in AXES]
    sent = []

    def device(offset):
        return tuple(lax.rem(m + o, n) for m, o, n in zip(me, offset, counts))

    def negated(offset):
        return tuple((-o) % n for o, n in zip(offset, counts))

    peers = {slot for slot in slots if any(slot)}
    for axis, count in enumerate(counts):
        for step in range(1, count):
            peers.add(tuple(step if a == axis else 0 for a in range(3)))
    everyone = [o for o in itertools.product(*[range(n) for n in counts]) if any(o)]
    direct = len(everyone) < MOST_DIRECT
    peers = everyone if direct else sorted(peers)
    barrier = pltpu.get_barrier_semaphore()
    for peer in peers:
        pl.semaphore_signal(barrier, inc=1, device_id=device(peer), device_id_type=MESH_ID)
    pl.semaphore_wait(barrier, len(peers))

    def neighbour_copy(turn, number):
        return pltpu.make_async_remote_copy(
            src_ref=fbuf.at[turn - 1, 0] if turn else nbuf.at[0],
            dst_ref=fbuf.at[turn - 1, number] if turn else nbuf.at[number],
            send_sem=nsend.at[turn, number - 1],
            recv_sem=nrecv.at[turn, number - 1],
            device_id=device(negated(slots[number])),
            device_id_type=MESH_ID,
        )

    def send_round(turn):
        for number in sorted(range(1, len(slots)), key=lambda k: (slots[k][0] == 0, k)):
            copy = neighbour_copy(turn, number)
            copy.start()
            sent.append(copy)

    def wait_round(turn, off_x):
        for number in range(1, len(slots)):
            if slots[number][0] == off_x:
                neighbour_copy(turn, number).wait_recv()

    def sum_copy(turn, stage, step):
        axis = 2 - stage
        offset = tuple((-step) % counts[axis] if a == axis else 0 for a in range(3))
        return pltpu.make_async_remote_copy(
            src_ref=rbuf.at[turn, stage, 0],
            dst_ref=rbuf.at[turn, stage, step],
            send_sem=rsend.at[turn, stage, step - 1],
            recv_sem=rrecv.at[turn, stage, step - 1],
            device_id=device(offset),
            device_id_type=MESH_ID,
        )

    def send_sum(turn, stage, value):
        rbuf[turn, stage, 0] = value
        for step in range(1, counts[2 - stage]):
            copy = sum_copy(turn, stage, step)
            copy.start()
            sent.append(copy)

    def wait_sum(turn, stage):
        for step in range(1, counts[2 - stage]):
            sum_copy(turn, stage, step).wait_recv()
        total = rbuf[turn, stage, 0]
        for step in range(1, counts[2 - stage]):
            total = total + rbuf[turn, stage, step]
        return total

    def put(turn, vector):
        for c in range(3):
            for part in range(cap // 128):
                fbuf[turn - 1, 0, pl.ds(c * (cap // 128) + part, 1), :] = vector[
                    c : c + 1, part * 128 : part * 128 + 128
                ]

    def taken(turn, number, c):
        each = cap // 128
        return jnp.concatenate(
            [fbuf[turn - 1, number, pl.ds(c * each + part, 1), :] for part in range(each)], axis=1
        )

    def direct_copy(number):
        return pltpu.make_async_remote_copy(
            src_ref=dbuf.at[0],
            dst_ref=dbuf.at[number + 1],
            send_sem=dsend.at[number],
            recv_sem=drecv.at[number],
            device_id=device(negated(everyone[number])),
            device_id_type=MESH_ID,
        )

    def sum_directly(value):
        dbuf[0] = value
        for number in range(len(everyone)):
            copy = direct_copy(number)
            copy.start()
            sent.append(copy)
        for number in range(len(everyone)):
            direct_copy(number).wait_recv()
        return jnp.sum(dbuf[...], axis=0)

    offs_y = sorted({1 % counts[1], (-1) % counts[1]})
    offs_z = sorted({1 % counts[2], (-1) % counts[2]})

    def halo_copy(number, source, target, offset):
        return pltpu.make_async_remote_copy(
            src_ref=source,
            dst_ref=target,
            send_sem=hsend.at[number],
            recv_sem=hrecv.at[number],
            device_id=device(negated(offset)),
            device_id_type=MESH_ID,
        )

    def go(copies):
        for copy in copies:
            copy.start()
            sent.append(copy)

    low, high = pl.ds(0, LOW), pl.ds(LOW, HIGH)
    along_x = [
        halo_copy(0, block.at[:, pl.ds(size_x - LOW, LOW)], xbuf.at[:, low], (counts[0] - 1, 0, 0)),
        halo_copy(1, block.at[:, pl.ds(0, HIGH)], xbuf.at[:, high], (1, 0, 0)),
    ]
    along_y, relayed_y = [], []
    for k, off in enumerate(offs_y):
        here = (0, off, 0)
        along_y.append(halo_copy(2 + k, block, ybuf.at[k, :, pl.ds(LOW, size_x)], here))
        relayed_y.append(halo_copy(4 + k, xbuf.at[:, low], ybuf.at[k, :, low], here))
        relayed_y.append(
            halo_copy(6 + k, xbuf.at[:, high], ybuf.at[k, :, pl.ds(LOW + size_x, HIGH)], here)
        )
    along_z = [halo_copy(8 + k, zpack, zbuf.at[k], (0, 0, off)) for k, off in enumerate(offs_z)]

    def widen():
        for copy in along_y + relayed_y:
            copy.wait_recv()
        below = ybuf.at[offs_y.index((-1) % counts[1])]
        above = ybuf.at[offs_y.index(1 % counts[1])]
        lane = lax.broadcasted_iota(jnp.int32, (4, rows_y, size_z), 2)
        zero = jnp.zeros((4, rows_y - size_y - LOW - HIGH, size_z), jnp.float32)
        packed = jnp.zeros((4, rows_y, size_z), jnp.float32)
        for plane in range(wide_x):
            if plane < LOW:
                own = xbuf[:, plane]
            elif plane < LOW + size_x:
                own = block[:, plane - LOW]
            else:
                own = xbuf[:, plane - size_x]
            tall = jnp.concatenate(
                [below[:, plane][:, size_y - LOW :], own, above[:, plane][:, :HIGH], zero], axis=1
            )
            fields[:, plane, :, pl.ds(0, size_z)] = tall
            ends = jnp.where(lane < HIGH, tall, pltpu.roll(tall, LOW + HIGH, 2))
            at = 8 * plane
            inside = (lane >= at) & (lane < at + LOW + HIGH)
            packed = jnp.where(inside, pltpu.roll(ends, at, 2) if at else ends, packed)
        zpack[...] = packed
        go(along_z)
        for copy in along_z:
            copy.wait_recv()
        before = zbuf[offs_z.index((-1) % counts[2])]
        after = zbuf[offs_z.index(1 % counts[2])]
        for plane in range(wide_x):
            at = 8 * plane
            tall = pltpu.roll(fields[:, plane, :, pl.ds(0, size_z)], LOW, 2)
            first = pltpu.roll(before, (-(at + HIGH)) % size_z, 2)
            last = pltpu.roll(after, (LOW - at) % size_z, 2)
            fields[:, plane, :, pl.ds(0, size_z)] = jnp.where(lane < LOW, first, tall)
            tail = jnp.where(lane < LOW, tall, jnp.where(lane < LOW + HIGH, last, 0.0))
            fields[:, plane, :, pl.ds(size_z, lanes - size_z)] = tail

    go(along_x + along_y)
    nbuf[0] = marks[...]
    send_round(0)

    def build(xi, yi, zi):
        number = slots.index((groups[0][xi][0], groups[1][yi][0], groups[2][zi][0]))
        info = nbuf[number]
        cells = [info[k : k + 1] for k in range(3)]
        fours = [weights(info[k + 3 : k + 4]) for k in range(3)]
        block = (yi * len(groups[2]) + zi) * cap
        start, planes = span(groups[0][xi][1], size_x)
        first = start // 8 * 8
        tall = round_up(start + planes - first, 8)
        tab_x = table(cells[0], fours[0], groups[0][xi][1], size_x, float(first), tall)
        tab_y = table(cells[1], fours[1], groups[1][yi][1], size_y, 0.0, rows_y)
        for plane in range(planes):
            at = start - first + plane
            txy[xi, pl.ds(plane * rows_y, rows_y), pl.ds(block, cap)] = tab_x[at : at + 1] * tab_y
        shifts = groups[2][zi][1]
        start, planes = span(shifts, size_z)
        first = start // 16 * 16
        tall = round_up(start + planes - first, 16)
        tab_z = table(cells[2], fours[2], shifts, size_z, float(first), tall)
        high, low = split(tab_z)
        for ref, part in ((thi, high), (tlo, low)):
            if first:
                ref[xi, pl.ds(0, first), pl.ds(block, cap)] = jnp.zeros((first, cap), jnp.bfloat16)
            ref[xi, pl.ds(first, tall), pl.ds(block, cap)] = part
            rest = lanes - first - tall
            if rest:
                ref[xi, pl.ds(first + tall, rest), pl.ds(block, cap)] = jnp.zeros(
                    (rest, cap), jnp.bfloat16
                )

    start_own, planes_own = span(groups[0][0][1], size_x)

    def interpolate(field):
        rows = planes_own * rows_y
        high, low = split(field.reshape(3 * rows, lanes))
        z_high, z_low = thi[0, :, pl.ds(0, cap)], tlo[0, :, pl.ds(0, cap)]
        part = dot_nn(high, z_high) + dot_nn(low, z_high) + dot_nn(high, z_low)
        plane = txy[0, pl.ds(0, rows), pl.ds(0, cap)]
        return jnp.concatenate(
            [
                jnp.sum(part[c * rows : (c + 1) * rows] * plane, axis=0, keepdims=True)
                for c in range(3)
            ],
            axis=0,
        )

    def spread(turn):
        for xi, (off_x, shifts) in enumerate(groups[0]):
            start, planes = span(shifts, size_x)
            rows = planes * rows_y
            wait_round(turn, off_x)
            for yi, (off_y, _) in enumerate(groups[1]):
                for zi, (off_z, _) in enumerate(groups[2]):
                    number = slots.index((off_x, off_y, off_z))
                    block = (yi * len(groups[2]) + zi) * cap
                    plane = txy[xi, pl.ds(0, rows), pl.ds(block, cap)]
                    for c in range(3):
                        high, low = split(plane * taken(turn, number, c))
                        whi[pl.ds(c * rows, rows), pl.ds(block, cap)] = high
                        wlo[pl.ds(c * rows, rows), pl.ds(block, cap)] = low
            high, low = whi[pl.ds(0, 3 * rows), :], wlo[pl.ds(0, 3 * rows), :]
            part = dot_nt(high, thi[xi]) + dot_nt(low, thi[xi]) + dot_nt(high, tlo[xi])
            part = part.reshape(3, planes, rows_y, lanes)
            if xi == 0:
                if start > 0:
                    grid[:, pl.ds(0, start)] = jnp.zeros((3, start, rows_y, lanes), jnp.float32)
                rest = wide_x - start - planes
                if rest > 0:
                    grid[:, pl.ds(start + planes, rest)] = jnp.zeros(
                        (3, rest, rows_y, lanes), jnp.float32
                    )
                grid[:, pl.ds(start, planes)] = part
            else:
                grid[:, pl.ds(start, planes)] += part

    def shifted(value, by, axis):
        return pltpu.roll(value, by % value.shape[axis], axis)

    def both(value, axis):
        return shifted(value, -1, axis), shifted(value, 1, axis)

    def add(value, axis):
        up, down = both(value, axis)
        return up + down

    def sub(value, axis):
        up, down = both(value, axis)
        return up - down

    def respond():
        scale = fields[3]
        mx, my, mz = (scale * grid[c] for c in range(3))
        slope_y, slope_z = sub(my, 1), sub(mz, 2)
        sum_x = 2.0 * mx + add(mx, 1) + add(mx, 2)
        slope = slope_y + slope_z
        px = sum_x[2:] + sum_x[:-2] + slope[2:] - slope[:-2]
        slope_x = mx[2:] - mx[:-2]
        sum_y = (2.0 * my + add(my, 2))[1:-1] + my[2:] + my[:-2]
        py = add(sum_y, 1) + sub(slope_x + slope_z[1:-1], 1)
        sum_z = (2.0 * mz + add(mz, 1))[1:-1] + mz[2:] + mz[:-2]
        pz = add(sum_z, 2) + sub(slope_x + slope_y[1:-1], 2)
        half = scale[1:-1] * 0.5
        return jnp.stack(
            [half * (m[1:-1] + p * (1.0 / 12.0)) for m, p in ((mx, px), (my, py), (mz, pz))]
        )

    target, stiffness, live = aux[pl.ds(0, 3), :], aux[pl.ds(3, 1), :], aux[pl.ds(4, 1), :]

    def apply(turn, vector, summing=None):
        spread(turn)
        if summing is not None:
            send_sum(summing, 1, wait_sum(summing, 0))
        field = respond()
        if summing is not None:
            send_sum(summing, 2, wait_sum(summing, 1))
        return live * (interpolate(field) + stiffness * vector)

    def partial_sums(residual, image):
        folded = []
        for other in (residual, image):
            row = jnp.sum(residual * other, axis=0, keepdims=True)
            total = row[:, :128]
            for at in range(128, cap, 128):
                total = total + row[:, at : at + 128]
            folded.append(total)
        return jnp.concatenate(folded, axis=0)

    def totals(tile):
        return (
            jnp.sum(tile[0:1], axis=1, keepdims=True),
            jnp.sum(tile[1:2], axis=1, keepdims=True),
        )

    build(0, 0, 0)
    for copy in along_x:
        copy.wait_recv()
    go(relayed_y)
    for off_x, _ in groups[0]:
        wait_round(0, off_x)
    for xi, yi, zi in itertools.product(*[range(len(group)) for group in groups]):
        if (xi, yi, zi) != (0, 0, 0):
            build(xi, yi, zi)
    widen()
    residual = live * (target - interpolate(fields[pl.ds(0, 3), pl.ds(1, size_x + 3)]))
    put(1, residual)
    send_round(1)

    image = apply(1, residual)
    direction, along, along_image = residual, image, None
    answer = None
    norm_before = alpha = None
    for step in range(ITERS):
        sums = partial_sums(residual, image)
        if step + 1 < ITERS or not direct:
            send_sum(step, 0, sums)
        if step + 1 < ITERS:
            put(step + 2, image)
            send_round(step + 2)
            ahead = apply(step + 2, image, step)
            norm, product = totals(wait_sum(step, 2))
        elif direct:
            norm, product = totals(sum_directly(sums))
        else:
            send_sum(step, 1, wait_sum(step, 0))
            send_sum(step, 2, wait_sum(step, 1))
            norm, product = totals(wait_sum(step, 2))
        if step == 0:
            alpha = norm / product
            along_image = ahead
        else:
            ratio = norm / norm_before
            alpha = norm / (product - ratio * norm / alpha)
            direction = residual + ratio * direction
            if step + 1 < ITERS:
                along = image + ratio * along
                along_image = ahead + ratio * along_image
        answer = alpha * direction if answer is None else answer + alpha * direction
        norm_before = norm
        if step + 1 < ITERS:
            residual = residual - alpha * along
            image = image - alpha * along_image
    out[...] = answer
    for copy in sent:
        copy.wait_send()


def body(mesh_counts, density, base_velocity, cells, offsets, target, stiffness, counts):
    sizes = density.shape
    size_x, size_y, size_z = sizes
    cap = cells.shape[1]
    rows_y, lanes = round_up(size_y + 5, 16), round_up(size_z + 5, 128)
    anchor = jnp.stack([lax.axis_index(name) * size for name, size in zip(AXES, sizes)])
    local = (cells - anchor[:, None]).astype(jnp.float32)
    marks = jnp.concatenate([local, offsets, jnp.zeros((2, cap), jnp.float32)], axis=0)
    live = (jnp.arange(cap, dtype=jnp.int32) < counts[0]).astype(jnp.float32)
    aux = jnp.concatenate(
        [target, stiffness[None], live[None], jnp.zeros((3, cap), jnp.float32)], axis=0
    )
    stacked = jnp.concatenate([base_velocity, lax.rsqrt(density)[None]], axis=0)
    groups = [axis_groups(count) for count in mesh_counts]
    number = len(groups[0]) * len(groups[1]) * len(groups[2])
    width = len(groups[1]) * len(groups[2]) * cap
    tallest = max(span(shifts, size_x)[1] for _, shifts in groups[0])
    longest = max(mesh_counts)
    turns = ITERS + 1
    devices = mesh_counts[0] * mesh_counts[1] * mesh_counts[2]
    most = devices if devices <= MOST_DIRECT else 1
    return pl.pallas_call(
        functools.partial(kernel, mesh_counts, sizes),
        out_shape=jax.ShapeDtypeStruct((3, cap), jnp.float32),
        in_specs=[pl.BlockSpec(memory_space=pltpu.VMEM)] * 3,
        out_specs=pl.BlockSpec(memory_space=pltpu.VMEM),
        scratch_shapes=[
            pltpu.VMEM((4, size_x + 5, rows_y, lanes), jnp.float32),
            pltpu.VMEM((4, LOW + HIGH, size_y, size_z), jnp.float32),
            pltpu.VMEM((2, 4, size_x + 5, size_y, size_z), jnp.float32),
            pltpu.VMEM((4, rows_y, size_z), jnp.float32),
            pltpu.VMEM((2, 4, rows_y, size_z), jnp.float32),
            pltpu.VMEM((number, 8, cap), jnp.float32),
            pltpu.VMEM((ITERS, number, 3 * (cap // 128), 128), jnp.float32),
            pltpu.VMEM((ITERS, 3, longest, 2, 128), jnp.float32),
            pltpu.VMEM((most, 2, 128), jnp.float32),
            pltpu.VMEM((len(groups[0]), tallest * rows_y, width), jnp.float32),
            pltpu.VMEM((len(groups[0]), lanes, width), jnp.bfloat16),
            pltpu.VMEM((len(groups[0]), lanes, width), jnp.bfloat16),
            pltpu.VMEM((3 * tallest * rows_y, width), jnp.bfloat16),
            pltpu.VMEM((3 * tallest * rows_y, width), jnp.bfloat16),
            pltpu.VMEM((3, size_x + 5, rows_y, lanes), jnp.float32),
            pltpu.SemaphoreType.DMA((turns, number - 1)),
            pltpu.SemaphoreType.DMA((turns, number - 1)),
            pltpu.SemaphoreType.DMA((ITERS, 3, longest - 1)),
            pltpu.SemaphoreType.DMA((ITERS, 3, longest - 1)),
            pltpu.SemaphoreType.DMA((most,)),
            pltpu.SemaphoreType.DMA((most,)),
            pltpu.SemaphoreType.DMA((10,)),
            pltpu.SemaphoreType.DMA((10,)),
        ],
        compiler_params=pltpu.CompilerParams(
            collective_id=0, has_side_effects=True, vmem_limit_bytes=60 * 1024 * 1024
        ),
    )(stacked, marks, aux)


def solution(mesh):
    return jax.shard_map(
        functools.partial(body, tuple(mesh.shape[name] for name in AXES)),
        mesh=mesh,
        in_specs=(
            P("gx", "gy", "gz"),
            P(None, "gx", "gy", "gz"),
            P(None, ("gx", "gy", "gz")),
            P(None, ("gx", "gy", "gz")),
            P(None, ("gx", "gy", "gz")),
            P(("gx", "gy", "gz")),
            P(("gx", "gy", "gz")),
        ),
        out_specs=P(None, ("gx", "gy", "gz")),
        check_vma=False,
    )
```

```python
import functools
import itertools

import jax
import jax.numpy as jnp
from jax import lax
from jax.experimental import pallas as pl
from jax.experimental.pallas import tpu as pltpu
from jax.sharding import PartitionSpec as P

ITERS = 3
MOST_DIRECT = 64
LOW, HIGH = 2, 3
MESH_ID = pl.DeviceIdType.MESH
AXES = ("gx", "gy", "gz")


def round_up(value, multiple):
    return -(-value // multiple) * multiple


def axis_groups(count):
    groups = {}
    for shift in (0, -1, 1):
        groups.setdefault(shift % count, []).append(shift)
    return list(groups.items())


def span(shifts, size):
    if shifts == [0]:
        return 1, size + 3
    if shifts == [-1]:
        return 0, 4
    if shifts == [1]:
        return size + 1, 4
    return 0, size + 5


def weights(fraction):
    root = jnp.sqrt(1.0 + 4.0 * fraction - 4.0 * fraction * fraction)
    near, far = 3.0 - 2.0 * fraction, 1.0 + 2.0 * fraction
    return ((near - root) / 8.0, (near + root) / 8.0, (far + root) / 8.0, (far - root) / 8.0)


def table(cell, four, shifts, size, first, rows):
    place = lax.broadcasted_iota(jnp.int32, (rows, cell.shape[1]), 0).astype(jnp.float32) + first
    total = None
    for shift in shifts:
        apart = place - (cell + (1.0 + shift * size))
        part = jnp.where(apart == 3.0, four[3], 0.0)
        for number in (2, 1, 0):
            part = jnp.where(apart == float(number), four[number], part)
        total = part if total is None else total + part
    return total


def split(value):
    high = value.astype(jnp.bfloat16)
    return high, (value - high.astype(jnp.float32)).astype(jnp.bfloat16)


def dot_nt(a, b):
    return lax.dot_general(a, b, (((1,), (1,)), ((), ())), preferred_element_type=jnp.float32)


def dot_nn(a, b):
    return lax.dot_general(a, b, (((1,), (0,)), ((), ())), preferred_element_type=jnp.float32)


def kernel(
    counts, sizes, block, marks, aux, out, fields, xbuf, ybuf, zpack, zbuf, nbuf, fbuf, rbuf, dbuf, txy, thi, tlo, whi, wlo, grid,
    nsend, nrecv, rsend, rrecv, dsend, drecv, hsend, hrecv,
):
    size_x, size_y, size_z = sizes
    cap = marks.shape[1]
    rows_y, lanes = fields.shape[2], fields.shape[3]
    assert 8 * (size_x + 5) <= size_z == lanes - size_z
    wide_x = size_x + 5
    groups = [axis_groups(count) for count in counts]
    slots = list(itertools.product(*[[offset for offset, _ in group] for group in groups]))
    me = [lax.axis_index(name) for name in AXES]
    sent = []

    def device(offset):
        return tuple(lax.rem(m + o, n) for m, o, n in zip(me, offset, counts))

    def negated(offset):
        return tuple((-o) % n for o, n in zip(offset, counts))

    peers = {slot for slot in slots if any(slot)}
    for axis, count in enumerate(counts):
        for step in range(1, count):
            peers.add(tuple(step if a == axis else 0 for a in range(3)))
    everyone = [o for o in itertools.product(*[range(n) for n in counts]) if any(o)]
    direct = len(everyone) < MOST_DIRECT
    peers = everyone if direct else sorted(peers)
    barrier = pltpu.get_barrier_semaphore()
    for peer in peers:
        pl.semaphore_signal(barrier, inc=1, device_id=device(peer), device_id_type=MESH_ID)
    pl.semaphore_wait(barrier, len(peers))

    def neighbour_copy(turn, number):
        return pltpu.make_async_remote_copy(
            src_ref=fbuf.at[turn - 1, 0] if turn else nbuf.at[0],
            dst_ref=fbuf.at[turn - 1, number] if turn else nbuf.at[number],
            send_sem=nsend.at[turn, number - 1],
            recv_sem=nrecv.at[turn, number - 1],
            device_id=device(negated(slots[number])),
            device_id_type=MESH_ID,
        )

    def send_round(turn):
        for number in sorted(range(1, len(slots)), key=lambda k: (slots[k][0] == 0, k)):
            copy = neighbour_copy(turn, number)
            copy.start()
            sent.append(copy)

    def wait_round(turn, off_x):
        for number in range(1, len(slots)):
            if slots[number][0] == off_x:
                neighbour_copy(turn, number).wait_recv()

    def sum_copy(turn, stage, step):
        axis = 2 - stage
        offset = tuple((-step) % counts[axis] if a == axis else 0 for a in range(3))
        return pltpu.make_async_remote_copy(
            src_ref=rbuf.at[turn, stage, 0],
            dst_ref=rbuf.at[turn, stage, step],
            send_sem=rsend.at[turn, stage, step - 1],
            recv_sem=rrecv.at[turn, stage, step - 1],
            device_id=device(offset),
            device_id_type=MESH_ID,
        )

    def send_sum(turn, stage, value):
        rbuf[turn, stage, 0] = value
        for step in range(1, counts[2 - stage]):
            copy = sum_copy(turn, stage, step)
            copy.start()
            sent.append(copy)

    def wait_sum(turn, stage):
        for step in range(1, counts[2 - stage]):
            sum_copy(turn, stage, step).wait_recv()
        total = rbuf[turn, stage, 0]
        for step in range(1, counts[2 - stage]):
            total = total + rbuf[turn, stage, step]
        return total

    def put(turn, vector):
        for c in range(3):
            for part in range(cap // 128):
                fbuf[turn - 1, 0, pl.ds(c * (cap // 128) + part, 1), :] = vector[
                    c : c + 1, part * 128 : part * 128 + 128
                ]

    def taken(turn, number, c):
        each = cap // 128
        return jnp.concatenate(
            [fbuf[turn - 1, number, pl.ds(c * each + part, 1), :] for part in range(each)], axis=1
        )

    def direct_copy(number):
        return pltpu.make_async_remote_copy(
            src_ref=dbuf.at[0],
            dst_ref=dbuf.at[number + 1],
            send_sem=dsend.at[number],
            recv_sem=drecv.at[number],
            device_id=device(negated(everyone[number])),
            device_id_type=MESH_ID,
        )

    def sum_directly(value):
        dbuf[0] = value
        for number in range(len(everyone)):
            copy = direct_copy(number)
            copy.start()
            sent.append(copy)
        for number in range(len(everyone)):
            direct_copy(number).wait_recv()
        return jnp.sum(dbuf[...], axis=0)

    offs_y = sorted({1 % counts[1], (-1) % counts[1]})
    offs_z = sorted({1 % counts[2], (-1) % counts[2]})

    def halo_copy(number, source, target, offset):
        return pltpu.make_async_remote_copy(
            src_ref=source,
            dst_ref=target,
            send_sem=hsend.at[number],
            recv_sem=hrecv.at[number],
            device_id=device(negated(offset)),
            device_id_type=MESH_ID,
        )

    def go(copies):
        for copy in copies:
            copy.start()
            sent.append(copy)

    low, high = pl.ds(0, LOW), pl.ds(LOW, HIGH)
    along_x = [
        halo_copy(0, block.at[:, pl.ds(size_x - LOW, LOW)], xbuf.at[:, low], (counts[0] - 1, 0, 0)),
        halo_copy(1, block.at[:, pl.ds(0, HIGH)], xbuf.at[:, high], (1, 0, 0)),
    ]
    along_y, relayed_y = [], []
    for k, off in enumerate(offs_y):
        here = (0, off, 0)
        along_y.append(halo_copy(2 + k, block, ybuf.at[k, :, pl.ds(LOW, size_x)], here))
        relayed_y.append(halo_copy(4 + k, xbuf.at[:, low], ybuf.at[k, :, low], here))
        relayed_y.append(
            halo_copy(6 + k, xbuf.at[:, high], ybuf.at[k, :, pl.ds(LOW + size_x, HIGH)], here)
        )
    along_z = [halo_copy(8 + k, zpack, zbuf.at[k], (0, 0, off)) for k, off in enumerate(offs_z)]

    def widen():
        for copy in along_y + relayed_y:
            copy.wait_recv()
        below = ybuf.at[offs_y.index((-1) % counts[1])]
        above = ybuf.at[offs_y.index(1 % counts[1])]
        lane = lax.broadcasted_iota(jnp.int32, (4, rows_y, size_z), 2)
        zero = jnp.zeros((4, rows_y - size_y - LOW - HIGH, size_z), jnp.float32)
        packed = jnp.zeros((4, rows_y, size_z), jnp.float32)
        for plane in range(wide_x):
            if plane < LOW:
                own = xbuf[:, plane]
            elif plane < LOW + size_x:
                own = block[:, plane - LOW]
            else:
                own = xbuf[:, plane - size_x]
            tall = jnp.concatenate(
                [below[:, plane][:, size_y - LOW :], own, above[:, plane][:, :HIGH], zero], axis=1
            )
            fields[:, plane, :, pl.ds(0, size_z)] = tall
            ends = jnp.where(lane < HIGH, tall, pltpu.roll(tall, LOW + HIGH, 2))
            at = 8 * plane
            inside = (lane >= at) & (lane < at + LOW + HIGH)
            packed = jnp.where(inside, pltpu.roll(ends, at, 2) if at else ends, packed)
        zpack[...] = packed
        go(along_z)
        for copy in along_z:
            copy.wait_recv()
        before = zbuf[offs_z.index((-1) % counts[2])]
        after = zbuf[offs_z.index(1 % counts[2])]
        for plane in range(wide_x):
            at = 8 * plane
            tall = pltpu.roll(fields[:, plane, :, pl.ds(0, size_z)], LOW, 2)
            first = pltpu.roll(before, (-(at + HIGH)) % size_z, 2)
            last = pltpu.roll(after, (LOW - at) % size_z, 2)
            fields[:, plane, :, pl.ds(0, size_z)] = jnp.where(lane < LOW, first, tall)
            tail = jnp.where(lane < LOW, tall, jnp.where(lane < LOW + HIGH, last, 0.0))
            fields[:, plane, :, pl.ds(size_z, lanes - size_z)] = tail

    go(along_x + along_y)
    nbuf[0] = marks[...]
    send_round(0)

    def build(xi, yi, zi):
        number = slots.index((groups[0][xi][0], groups[1][yi][0], groups[2][zi][0]))
        info = nbuf[number]
        cells = [info[k : k + 1] for k in range(3)]
        fours = [weights(info[k + 3 : k + 4]) for k in range(3)]
        block = (yi * len(groups[2]) + zi) * cap
        start, planes = span(groups[0][xi][1], size_x)
        first = start // 8 * 8
        tall = round_up(start + planes - first, 8)
        tab_x = table(cells[0], fours[0], groups[0][xi][1], size_x, float(first), tall)
        tab_y = table(cells[1], fours[1], groups[1][yi][1], size_y, 0.0, rows_y)
        for plane in range(planes):
            at = start - first + plane
            txy[xi, pl.ds(plane * rows_y, rows_y), pl.ds(block, cap)] = tab_x[at : at + 1] * tab_y
        shifts = groups[2][zi][1]
        start, planes = span(shifts, size_z)
        first = start // 16 * 16
        tall = round_up(start + planes - first, 16)
        tab_z = table(cells[2], fours[2], shifts, size_z, float(first), tall)
        high, low = split(tab_z)
        for ref, part in ((thi, high), (tlo, low)):
            if first:
                ref[xi, pl.ds(0, first), pl.ds(block, cap)] = jnp.zeros((first, cap), jnp.bfloat16)
            ref[xi, pl.ds(first, tall), pl.ds(block, cap)] = part
            rest = lanes - first - tall
            if rest:
                ref[xi, pl.ds(first + tall, rest), pl.ds(block, cap)] = jnp.zeros(
                    (rest, cap), jnp.bfloat16
                )

    start_own, planes_own = span(groups[0][0][1], size_x)

    def interpolate(field):
        rows = planes_own * rows_y
        high, low = split(field.reshape(3 * rows, lanes))
        z_high, z_low = thi[0, :, pl.ds(0, cap)], tlo[0, :, pl.ds(0, cap)]
        part = dot_nn(high, z_high) + dot_nn(low, z_high) + dot_nn(high, z_low)
        plane = txy[0, pl.ds(0, rows), pl.ds(0, cap)]
        return jnp.concatenate(
            [
                jnp.sum(part[c * rows : (c + 1) * rows] * plane, axis=0, keepdims=True)
                for c in range(3)
            ],
            axis=0,
        )

    def spread(turn):
        for xi, (off_x, shifts) in enumerate(groups[0]):
            start, planes = span(shifts, size_x)
            rows = planes * rows_y
            for yi, (off_y, _) in enumerate(groups[1]):
                for zi, (off_z, _) in enumerate(groups[2]):
                    number = slots.index((off_x, off_y, off_z))
                    if number:
                        neighbour_copy(turn, number).wait_recv()
                    block = (yi * len(groups[2]) + zi) * cap
                    plane = txy[xi, pl.ds(0, rows), pl.ds(block, cap)]
                    for c in range(3):
                        high, low = split(plane * taken(turn, number, c))
                        whi[pl.ds(c * rows, rows), pl.ds(block, cap)] = high
                        wlo[pl.ds(c * rows, rows), pl.ds(block, cap)] = low
            high, low = whi[pl.ds(0, 3 * rows), :], wlo[pl.ds(0, 3 * rows), :]
            part = dot_nt(high, thi[xi]) + dot_nt(low, thi[xi]) + dot_nt(high, tlo[xi])
            part = part.reshape(3, planes, rows_y, lanes)
            if xi == 0:
                if start > 0:
                    grid[:, pl.ds(0, start)] = jnp.zeros((3, start, rows_y, lanes), jnp.float32)
                rest = wide_x - start - planes
                if rest > 0:
                    grid[:, pl.ds(start + planes, rest)] = jnp.zeros(
                        (3, rest, rows_y, lanes), jnp.float32
                    )
                grid[:, pl.ds(start, planes)] = part
            else:
                grid[:, pl.ds(start, planes)] += part

    def shifted(value, by, axis):
        return pltpu.roll(value, by % value.shape[axis], axis)

    def both(value, axis):
        return shifted(value, -1, axis), shifted(value, 1, axis)

    def add(value, axis):
        up, down = both(value, axis)
        return up + down

    def sub(value, axis):
        up, down = both(value, axis)
        return up - down

    def respond():
        scale = fields[3]
        mx, my, mz = (scale * grid[c] for c in range(3))
        slope_y, slope_z = sub(my, 1), sub(mz, 2)
        sum_x = 2.0 * mx + add(mx, 1) + add(mx, 2)
        slope = slope_y + slope_z
        px = sum_x[2:] + sum_x[:-2] + slope[2:] - slope[:-2]
        slope_x = mx[2:] - mx[:-2]
        sum_y = (2.0 * my + add(my, 2))[1:-1] + my[2:] + my[:-2]
        py = add(sum_y, 1) + sub(slope_x + slope_z[1:-1], 1)
        sum_z = (2.0 * mz + add(mz, 1))[1:-1] + mz[2:] + mz[:-2]
        pz = add(sum_z, 2) + sub(slope_x + slope_y[1:-1], 2)
        half = scale[1:-1] * 0.5
        return jnp.stack(
            [half * (m[1:-1] + p * (1.0 / 12.0)) for m, p in ((mx, px), (my, py), (mz, pz))]
        )

    target, stiffness, live = aux[pl.ds(0, 3), :], aux[pl.ds(3, 1), :], aux[pl.ds(4, 1), :]

    def apply(turn, vector, summing=None):
        spread(turn)
        if summing is not None:
            send_sum(summing, 1, wait_sum(summing, 0))
        field = respond()
        if summing is not None:
            send_sum(summing, 2, wait_sum(summing, 1))
        return live * (interpolate(field) + stiffness * vector)

    def partial_sums(residual, image):
        folded = []
        for other in (residual, image):
            row = jnp.sum(residual * other, axis=0, keepdims=True)
            total = row[:, :128]
            for at in range(128, cap, 128):
                total = total + row[:, at : at + 128]
            folded.append(total)
        return jnp.concatenate(folded, axis=0)

    def totals(tile):
        return (
            jnp.sum(tile[0:1], axis=1, keepdims=True),
            jnp.sum(tile[1:2], axis=1, keepdims=True),
        )

    build(0, 0, 0)
    for copy in along_x:
        copy.wait_recv()
    go(relayed_y)
    for off_x, _ in groups[0]:
        wait_round(0, off_x)
    for xi, yi, zi in itertools.product(*[range(len(group)) for group in groups]):
        if (xi, yi, zi) != (0, 0, 0):
            build(xi, yi, zi)
    widen()
    residual = live * (target - interpolate(fields[pl.ds(0, 3), pl.ds(1, size_x + 3)]))
    put(1, residual)
    send_round(1)

    image = apply(1, residual)
    direction, along, along_image = residual, image, None
    answer = None
    norm_before = alpha = None
    for step in range(ITERS):
        sums = partial_sums(residual, image)
        if step + 1 < ITERS or not direct:
            send_sum(step, 0, sums)
        if step + 1 < ITERS:
            put(step + 2, image)
            send_round(step + 2)
            ahead = apply(step + 2, image, step)
            norm, product = totals(wait_sum(step, 2))
        elif direct:
            norm, product = totals(sum_directly(sums))
        else:
            send_sum(step, 1, wait_sum(step, 0))
            send_sum(step, 2, wait_sum(step, 1))
            norm, product = totals(wait_sum(step, 2))
        if step == 0:
            alpha = norm / product
            along_image = ahead
        else:
            ratio = norm / norm_before
            alpha = norm / (product - ratio * norm / alpha)
            direction = residual + ratio * direction
            if step + 1 < ITERS:
                along = image + ratio * along
                along_image = ahead + ratio * along_image
        answer = alpha * direction if answer is None else answer + alpha * direction
        norm_before = norm
        if step + 1 < ITERS:
            residual = residual - alpha * along
            image = image - alpha * along_image
    out[...] = answer
    for copy in sent:
        copy.wait_send()


def body(mesh_counts, density, base_velocity, cells, offsets, target, stiffness, counts):
    sizes = density.shape
    size_x, size_y, size_z = sizes
    cap = cells.shape[1]
    rows_y, lanes = round_up(size_y + 5, 16), round_up(size_z + 5, 128)
    anchor = jnp.stack([lax.axis_index(name) * size for name, size in zip(AXES, sizes)])
    local = (cells - anchor[:, None]).astype(jnp.float32)
    marks = jnp.concatenate([local, offsets, jnp.zeros((2, cap), jnp.float32)], axis=0)
    live = (jnp.arange(cap, dtype=jnp.int32) < counts[0]).astype(jnp.float32)
    aux = jnp.concatenate(
        [target, stiffness[None], live[None], jnp.zeros((3, cap), jnp.float32)], axis=0
    )
    stacked = jnp.concatenate([base_velocity, lax.rsqrt(density)[None]], axis=0)
    groups = [axis_groups(count) for count in mesh_counts]
    number = len(groups[0]) * len(groups[1]) * len(groups[2])
    width = len(groups[1]) * len(groups[2]) * cap
    tallest = max(span(shifts, size_x)[1] for _, shifts in groups[0])
    longest = max(mesh_counts)
    turns = ITERS + 1
    devices = mesh_counts[0] * mesh_counts[1] * mesh_counts[2]
    most = devices if devices <= MOST_DIRECT else 1
    return pl.pallas_call(
        functools.partial(kernel, mesh_counts, sizes),
        out_shape=jax.ShapeDtypeStruct((3, cap), jnp.float32),
        in_specs=[pl.BlockSpec(memory_space=pltpu.VMEM)] * 3,
        out_specs=pl.BlockSpec(memory_space=pltpu.VMEM),
        scratch_shapes=[
            pltpu.VMEM((4, size_x + 5, rows_y, lanes), jnp.float32),
            pltpu.VMEM((4, LOW + HIGH, size_y, size_z), jnp.float32),
            pltpu.VMEM((2, 4, size_x + 5, size_y, size_z), jnp.float32),
            pltpu.VMEM((4, rows_y, size_z), jnp.float32),
            pltpu.VMEM((2, 4, rows_y, size_z), jnp.float32),
            pltpu.VMEM((number, 8, cap), jnp.float32),
            pltpu.VMEM((ITERS, number, 3 * (cap // 128), 128), jnp.float32),
            pltpu.VMEM((ITERS, 3, longest, 2, 128), jnp.float32),
            pltpu.VMEM((most, 2, 128), jnp.float32),
            pltpu.VMEM((len(groups[0]), tallest * rows_y, width), jnp.float32),
            pltpu.VMEM((len(groups[0]), lanes, width), jnp.bfloat16),
            pltpu.VMEM((len(groups[0]), lanes, width), jnp.bfloat16),
            pltpu.VMEM((3 * tallest * rows_y, width), jnp.bfloat16),
            pltpu.VMEM((3 * tallest * rows_y, width), jnp.bfloat16),
            pltpu.VMEM((3, size_x + 5, rows_y, lanes), jnp.float32),
            pltpu.SemaphoreType.DMA((turns, number - 1)),
            pltpu.SemaphoreType.DMA((turns, number - 1)),
            pltpu.SemaphoreType.DMA((ITERS, 3, longest - 1)),
            pltpu.SemaphoreType.DMA((ITERS, 3, longest - 1)),
            pltpu.SemaphoreType.DMA((most,)),
            pltpu.SemaphoreType.DMA((most,)),
            pltpu.SemaphoreType.DMA((10,)),
            pltpu.SemaphoreType.DMA((10,)),
        ],
        compiler_params=pltpu.CompilerParams(
            collective_id=0, has_side_effects=True, vmem_limit_bytes=60 * 1024 * 1024
        ),
    )(stacked, marks, aux)


def solution(mesh):
    return jax.shard_map(
        functools.partial(body, tuple(mesh.shape[name] for name in AXES)),
        mesh=mesh,
        in_specs=(
            P("gx", "gy", "gz"),
            P(None, "gx", "gy", "gz"),
            P(None, ("gx", "gy", "gz")),
            P(None, ("gx", "gy", "gz")),
            P(None, ("gx", "gy", "gz")),
            P(("gx", "gy", "gz")),
            P(("gx", "gy", "gz")),
        ),
        out_specs=P(None, ("gx", "gy", "gz")),
        check_vma=False,
    )
```
